32 devices in a mesh: attn: 8 (over z, x), expert: 4 (over y, core).
Axes of the slice: x: 2, y: 2, z: 4, core: 2. Of those that a mesh axis runs over, the one named last changes fastest.
Arguments:
- resid: bfloat16 [512, 6144], P('attn', 'expert')
- query: bfloat16 [512, 6144], P('attn', 'expert'), may hold values from -1 to 1
- key_cache: bfloat16 [512, 8, 128, 128], P('attn', 'expert'), may hold values from -4 to 4
- value_cache: bfloat16 [512, 8, 128, 128], P('attn', 'expert'), may hold values from -6 to 6
- new_key: bfloat16 [512, 1024], P('attn', 'expert'), may hold values from -4 to 4
- new_value: bfloat16 [512, 1024], P('attn', 'expert'), may hold values from -6 to 6
- lengths: int32 [512], P('attn'), may hold values from 1 to 128, as said below
- norm_gain: float32 [6144], P('expert'), may hold values from 0.1 to 1.9
- router_weight: float32 [6144, 8], P('expert'), may hold values from -0.078125 to 0.078125
- expert_ids: int32 [512, 2], P('attn'), may hold values from 0 to 7, as said below
- w_gate: bfloat16 [8, 6144, 8192], P('expert', None, 'attn'), may hold values from -0.078125 to 0.078125
- w_up: bfloat16 [8, 6144, 8192], P('expert', None, 'attn'), may hold values from -0.078125 to 0.078125
- w_down: bfloat16 [8, 8192, 6144], P('expert', 'attn'), may hold values from -0.0625 to 0.0625
Outputs:
- layer_out: bfloat16 [512, 6144], P('attn', 'expert')
The draws below stay inside these ranges and needn't reach their ends.
Inputs may be any that keep to these rules, and one draw needn't show every extreme that they name: `expert_ids`: each row names two different experts. Within each aligned block of 64 rows (the rows of one index of attn) no expert is named by more than 32 rows, and one expert, the same in every block, is named by exactly 32 rows in each block. `lengths`: some row has all 128 positions filled and some row has one.
All inputs are finite; a program needn't handle non-finite values.
Results may differ from the reference program's by a relative error of at most 0.0095.
Values may be sent and summed in bfloat16 or wider, within the bound.
A program may use at most 128 MiB of HBM per device.

```python
import math
import jax
import jax.numpy as jnp
from jax import lax

D = 6144
HQ = 48
KVH = 8
HD = 128
E = 8
FF = 8192
R_DEV = 64
CACHE = 128
CAP = 32
ROWS = 512
N_ATTN = 8


def draw_resid(key, part):
    key_base, key_rows, key_cols = jax.random.split(key, 3)
    position = jnp.arange(D, dtype=jnp.float32)[None, :] / (D - 1)
    base = jnp.clip(jax.random.normal(key_base, (ROWS, D), jnp.float32), -6.0, 6.0)
    rising = jnp.exp(position * math.log(3.0))
    row_scale = jnp.exp(jax.random.uniform(key_rows, (ROWS, 1), jnp.float32, math.log(0.5), math.log(2.0)))
    factor = 0.15
    spread = jnp.exp(jax.random.uniform(key_cols, (1, D), jnp.float32, 0.0, math.log(3.4)))
    return (factor * base * rising * spread * row_scale).astype(jnp.bfloat16)


def draw_lengths(key, part):
    key_all, key_full, key_short = jax.random.split(key, 3)
    filled = jax.random.randint(key_all, (ROWS,), 1, CACHE + 1)
    full_row = jax.random.randint(key_full, (), 0, ROWS)
    short_row = (full_row + 1 + jax.random.randint(key_short, (), 0, ROWS - 1)) % ROWS
    filled = filled.at[full_row].set(CACHE)
    filled = filled.at[short_row].set(1)
    return filled.astype(jnp.int32)


def draw_expert_ids(key, part):
    key_hot, key_rows, key_order, key_flip = jax.random.split(key, 4)
    block_count = ROWS // R_DEV
    hot_expert = jax.random.randint(key_hot, (), 0, E)
    position = jax.vmap(lambda sub_key: jax.random.permutation(sub_key, R_DEV))(jax.random.split(key_rows, block_count))
    ordering = jax.vmap(lambda sub_key: jax.random.permutation(sub_key, E - 1))(jax.random.split(key_order, block_count))
    others = ordering + (ordering >= hot_expert).astype(jnp.int32)
    first_other = jnp.take_along_axis(others, position % (E - 1), axis=1)
    next_other = jnp.take_along_axis(others, (position + 1) % (E - 1), axis=1)
    leading = position < CAP
    choice_one = jnp.where(leading, hot_expert, first_other)
    choice_two = jnp.where(leading, first_other, next_other)
    flipped = jax.random.randint(key_flip, (block_count, R_DEV), 0, 2) == 1
    column_a = jnp.where(flipped, choice_two, choice_one)
    column_b = jnp.where(flipped, choice_one, choice_two)
    return jnp.stack([column_a, column_b], axis=-1).reshape(ROWS, 2).astype(jnp.int32)


def steps_of(own_key, shape, shards, low, high):
    factor_of = 1.0
    for dim, parts in shards:
        steps = jax.random.uniform(jax.random.fold_in(jax.random.fold_in(own_key, 6), dim), (parts,), jnp.float32, low / len(shards), high / len(shards))
        factor_of = factor_of * jnp.repeat(jnp.exp(steps), shape[dim] // parts).reshape((-1,) + (1,) * (len(shape) - 1 - dim))
    return factor_of


def centred(stream_key, shape, scale, bound, pieces=(), held_as=jnp.bfloat16):
    values = scale * jax.random.normal(stream_key, shape, jnp.float32)
    if pieces:
        values = values * steps_of(stream_key, shape, pieces, -0.22, 0.18)
    return jnp.clip(values, -bound, bound).astype(held_as)


def setup_inputs(seed: int = 0) -> dict:
    splits = jax.random.split(jax.random.key(seed), 14)
    return {
        "resid": draw_resid(jax.random.fold_in(splits[13], 71), 0),
        "query": jnp.clip(jax.random.uniform(splits[1], (ROWS, D), jnp.float32, -1.0, 1.0) * steps_of(splits[1], (ROWS, D), ((0, 8), (1, 4)), -0.4, 0.0), -1.0, 1.0).astype(jnp.bfloat16),
        "key_cache": centred(splits[2], (ROWS, KVH, CACHE, HD), 1.0, 4.0, ((0, 8), (1, 4))),
        "value_cache": centred(splits[3], (ROWS, KVH, CACHE, HD), 1.0, 6.0, ((0, 8), (1, 4))),
        "new_key": centred(splits[4], (ROWS, KVH * HD), 1.0, 4.0, ((0, 8), (1, 4))),
        "new_value": centred(splits[5], (ROWS, KVH * HD), 1.0, 6.0, ((0, 8), (1, 4))),
        "lengths": draw_lengths(jax.random.fold_in(splits[13], 71), 0),
        "norm_gain": jnp.clip(1.0 + 0.18 * jax.random.normal(splits[7], (D,), jnp.float32), 0.1, 1.9),
        "router_weight": centred(splits[8], (D, E), D ** -0.5, 0.078125, ((0, 4),), jnp.float32),
        "expert_ids": draw_expert_ids(jax.random.fold_in(splits[13], 71), 0),
        "w_gate": centred(splits[10], (E, D, FF), D ** -0.5, 0.078125, ((0, 4), (2, 8))),
        "w_up": centred(splits[11], (E, D, FF), D ** -0.5, 0.078125, ((0, 4), (2, 8))),
        "w_down": centred(splits[12], (E, FF, D), FF ** -0.5, 0.0625, ((0, 4), (1, 8))),
    }


EPSILON = 1e-05

def reference(resid, query, key_cache, value_cache, new_key, new_value, lengths, norm_gain, router_weight, expert_ids, w_gate, w_up, w_down):
    row_count = resid.shape[0]
    group_size = HQ // KVH
    score_scale = 1.0 / math.sqrt(HD)
    queries = query.astype(jnp.float32).reshape(row_count, KVH, group_size, HD)
    scores = jnp.einsum('rkgd,rkld->rkgl', queries, key_cache.astype(jnp.float32)) * score_scale
    fresh_score = jnp.einsum('rkgd,rkd->rkg', queries, new_key.astype(jnp.float32).reshape(row_count, KVH, HD)) * score_scale
    usable = jnp.arange(CACHE, dtype=jnp.int32)[None, :] < lengths[:, None]
    powers = jnp.where(usable[:, None, None, :], jnp.exp(scores), jnp.float32(0.0))
    fresh_power = jnp.exp(fresh_score)
    denominator = lax.optimization_barrier(jnp.sum(powers, axis=-1)) + fresh_power
    weights_cache = (powers / denominator[..., None]).astype(jnp.bfloat16)
    weight_fresh = (fresh_power / denominator).astype(jnp.bfloat16)
    attended = jnp.einsum('rkgl,rkld->rkgd', weights_cache.astype(jnp.float32), value_cache.astype(jnp.float32))
    attended = attended + weight_fresh.astype(jnp.float32)[..., None] * new_value.astype(jnp.float32).reshape(row_count, KVH, 1, HD)
    hidden_state = resid.astype(jnp.float32) + attended.reshape(row_count, D)
    mean_square = lax.optimization_barrier(jnp.mean(hidden_state * hidden_state, axis=1, keepdims=True))
    normed = hidden_state * lax.rsqrt(mean_square + EPSILON) * norm_gain
    narrow = normed.astype(jnp.bfloat16)
    logits = jnp.dot(normed, router_weight, precision=lax.Precision.HIGHEST)
    choose = expert_ids[:, :, None] == jnp.arange(E, dtype=jnp.int32)[None, None, :]
    picked = lax.optimization_barrier(jnp.sum(jnp.where(choose, logits[:, None, :], jnp.float32(0.0)), axis=2))
    first_weight = 1.0 / (1.0 + jnp.exp(picked[:, 1] - picked[:, 0]))
    second_weight = 1.0 / (1.0 + jnp.exp(picked[:, 0] - picked[:, 1]))
    hits = lax.optimization_barrier(jnp.sum(choose.astype(jnp.int32), axis=1)).reshape(row_count // R_DEV, R_DEV, E)
    before = (jnp.cumsum(hits, axis=1) - hits).reshape(row_count, E)
    slot_index = lax.optimization_barrier(jnp.sum(jnp.where(choose, before[:, None, :], 0), axis=2)).astype(jnp.int32)
    block_index = (jnp.arange(row_count, dtype=jnp.int32) // R_DEV)[:, None]
    destination = (block_index * CAP + slot_index).astype(jnp.int32)
    owner = jnp.broadcast_to(jnp.arange(row_count, dtype=jnp.int32)[:, None], (row_count, 2))
    table = jnp.zeros((E, N_ATTN * CAP), jnp.int32).at[expert_ids, destination].set(owner)
    group_width = FF // N_ATTN

    def run_expert(packed):
        gate_matrix, up_matrix, down_matrix, row_index = packed
        taken = narrow[row_index]
        gate_part = jnp.dot(taken, gate_matrix, preferred_element_type=jnp.float32)
        up_part = jnp.dot(taken, up_matrix, preferred_element_type=jnp.float32)
        activation = (jax.nn.silu(gate_part) * up_part).astype(jnp.bfloat16)
        total = jnp.zeros((taken.shape[0], D), jnp.float32)
        for group in range(N_ATTN):
            partial_value = jnp.dot(activation[:, group * group_width:(group + 1) * group_width], down_matrix[group * group_width:(group + 1) * group_width], preferred_element_type=jnp.float32)
            total = total + partial_value.astype(jnp.bfloat16).astype(jnp.float32)
        return total.astype(jnp.bfloat16)
    outputs = lax.map(run_expert, (w_gate, w_up, w_down, table))
    first_out = outputs[expert_ids[:, 0], destination[:, 0]].astype(jnp.float32)
    second_out = outputs[expert_ids[:, 1], destination[:, 1]].astype(jnp.float32)
    total = hidden_state + first_weight[:, None] * first_out + second_weight[:, None] * second_out
    return total.astype(jnp.bfloat16)
```

```python
import functools
import math

import jax
import jax.numpy as jnp
from jax import lax
from jax.experimental import pallas as pl
from jax.experimental.pallas import tpu as pltpu
from jax.sharding import PartitionSpec as P

EPSILON = 1e-05
LANES = 128
CORES = 2
PARTS = 3
STAT = 16
MESH = pl.DeviceIdType.MESH


def grid_of(attn, expert):
    ny = max(expert // CORES, 1)
    nx = ny if attn % ny == 0 else 1
    return attn // nx, nx, ny


def halves_of(width):
    tiles = width // LANES
    first = (tiles - tiles // 2) * LANES
    return pl.ds(0, first), pl.ds(first, width - first)


class Place:
    def __init__(self, sizes):
        self.nz, self.nx, self.ny = sizes
        a = lax.axis_index("attn")
        e = lax.axis_index("expert")
        self.z, self.x = a // self.nx, lax.rem(a, self.nx)
        self.y, self.c = e // CORES, lax.rem(e, CORES)

    def device(self, z=None, x=None, y=None, c=None):
        z = self.z if z is None else z
        x = self.x if x is None else x
        y = self.y if y is None else y
        c = self.c if c is None else c
        return (z * self.nx + x, y * CORES + c)

    def greet(self):
        barrier = pltpu.get_barrier_semaphore()
        count = jnp.int32(1)

        def signal(dev):
            pl.semaphore_signal(barrier, inc=1, device_id=dev, device_id_type=MESH)

        signal(self.device(c=1 - self.c))
        for name, p, n in (("z", self.z, self.nz), ("x", self.x, self.nx), ("y", self.y, self.ny)):
            for step in (-1, 1):
                inside = jnp.logical_and(p + step >= 0, p + step < n)
                pl.when(inside)(functools.partial(signal, self.device(**{name: p + step})))
                count = count + inside.astype(jnp.int32)
        pl.semaphore_wait(barrier, count)


def gather_kernel(sizes, x_ref, g_ref, local_sem, z_send, z_recv, p1_send, p1_recv, p2_send, p2_recv, s_send, s_recv):
    me = Place(sizes)
    nz, nx, ny = sizes
    z, x, y, c = me.z, me.x, me.y, me.c
    width = x_ref.shape[1]
    cols = halves_of(width)
    me.greet()
    started = []

    def send(cond, src, dst, ssem, rsem, dev):
        copy = pltpu.make_async_remote_copy(
            src_ref=src, dst_ref=dst, send_sem=ssem, recv_sem=rsem, device_id=dev, device_id_type=MESH
        )
        started.append((cond, copy))
        if cond is None:
            copy.start()
        else:
            pl.when(cond)(copy.start)

    def await_block(dst, ssem, rsem):
        pltpu.make_async_remote_copy(
            src_ref=dst, dst_ref=dst, send_sem=ssem, recv_sem=rsem,
            device_id=me.device(c=1 - c), device_id_type=MESH,
        ).wait_recv()

    def block(bz, bx, by, core=None):
        core = c if core is None else core
        return g_ref.at[bz * nx + bx, by * CORES + core]

    def half(ref, h):
        return ref.at[:, cols[h]]

    def to_sibling(cond, src, bz, bx, by, h):
        slot = (bz * nx + bx, by, h)
        send(cond, half(src, h), half(block(bz, bx, by), h), s_send.at[slot], s_recv.at[slot], me.device(c=1 - c))

    def line(h, stage):
        return ("x", x, nx) if (h == 0) == (stage == 0) else ("y", y, ny)

    def along(cond, src, dst, h, stage, step, way, slot):
        name, p, n = line(h, stage)
        to = p + 1 if way == 0 else p - 1
        inside = to < n if way == 0 else to >= 0
        ssem, rsem = (p1_send, p1_recv) if stage == 0 else (p2_send, p2_recv)
        index = (h, step, way) + slot
        cond = inside if cond is None else jnp.logical_and(cond, inside)
        send(cond, half(src, h), half(dst, h), ssem.at[index], rsem.at[index], me.device(**{name: to}))

    def spread(cond, src, bz):
        for h in range(2):
            for way in range(2):
                along(cond, src, block(bz, x, y), h, 0, 0, way, (bz,))
            to_sibling(cond, src, bz, x, y, h)

    def z_hop(cond, src, bz, step, way):
        to = z + 1 if way == 0 else z - 1
        inside = to < nz if way == 0 else to >= 0
        cond = inside if cond is None else jnp.logical_and(cond, inside)
        send(cond, src, block(bz, x, y), z_send.at[step, way], z_recv.at[step, way], me.device(z=to))

    for way in range(2):
        if nz > 1:
            z_hop(None, x_ref, z, 0, way)
    spread(None, x_ref, z)
    local = pltpu.make_async_copy(x_ref, block(z, x, y), local_sem)
    local.start()
    for step in range(1, nz):
        for way in range(2):
            bz = z - step if way == 0 else z + step
            have = bz >= 0 if way == 0 else bz < nz
            dst = block(bz, x, y)
            pl.when(have)(functools.partial(await_block, dst, z_send.at[step - 1, way], z_recv.at[step - 1, way]))
            if step < nz - 1:
                z_hop(have, dst, bz, step, way)
            spread(have, dst, bz)
    turn = jnp.where(z < nz // 2, 1, nz - 1)
    order = [lax.rem(z + k * turn, nz) for k in range(nz)]

    def second(cond, src, h, bz, other):
        for way in range(2):
            along(cond, src, src, h, 1, 0, way, (bz, other))

    local.wait()
    for bz in order:
        for h in range(2):
            second(None, block(bz, x, y), h, bz, line(h, 0)[1])
    for step in range(1, max(nx, ny)):
        for bz in order:
            for h in range(2):
                name, p, n = line(h, 0)
                if step >= n:
                    continue
                for way in range(2):
                    q = p - step if way == 0 else p + step
                    have = q >= 0 if way == 0 else q < n
                    bx, by = (q, y) if name == "x" else (x, q)
                    dst = block(bz, bx, by)
                    index = (h, step - 1, way, bz)
                    pl.when(have)(functools.partial(await_block, half(dst, h), p1_send.at[index], p1_recv.at[index]))
                    if step < n - 1:
                        along(have, dst, dst, h, 0, step, way, (bz,))
                    second(have, dst, h, bz, q)
                    to_sibling(have, dst, bz, bx, by, h)
    for step in range(1, max(nx, ny)):
        for k in range(max(nx, ny)):
            for bz in order:
                for h in range(2):
                    _, first_p, first_n = line(h, 0)
                    name, p, n = line(h, 1)
                    if step >= n or k >= first_n:
                        continue
                    other = lax.rem(first_p + k, first_n)
                    for way in range(2):
                        q = p - step if way == 0 else p + step
                        have = q >= 0 if way == 0 else q < n
                        bx, by = (q, other) if name == "x" else (other, q)
                        dst = block(bz, bx, by)
                        index = (h, step - 1, way, bz, other)
                        pl.when(have)(
                            functools.partial(await_block, half(dst, h), p2_send.at[index], p2_recv.at[index])
                        )
                        if step < n - 1:
                            along(have, dst, dst, h, 1, step, way, (bz, other))
                        to_sibling(have, dst, bz, bx, by, h)
    for bz in range(nz):
        for bx in range(nx):
            for by in range(ny):
                for h in range(2):
                    slot = (bz * nx + bx, by, h)
                    await_block(half(block(bz, bx, by, 1 - c), h), s_send.at[slot], s_recv.at[slot])
    for cond, copy in started:
        if cond is None:
            copy.wait_send()
        else:
            pl.when(cond)(copy.wait_send)


def gather_all(block, sizes):
    nz, nx, ny = sizes
    rows, width = block.shape
    wide = max(nx, ny)
    steps = max(wide - 1, 1)
    dma = pltpu.SemaphoreType.DMA
    stage = [dma((max(nz - 1, 1), 2))] * 2 + [dma((2, steps, 2, nz))] * 2
    stage += [dma((2, steps, 2, nz, wide))] * 2 + [dma((nz * nx, ny, 2))] * 2
    return pl.pallas_call(
        functools.partial(gather_kernel, sizes),
        out_shape=jax.ShapeDtypeStruct((nz * nx, ny * CORES, rows, width), block.dtype),
        in_specs=[pl.BlockSpec(memory_space=pltpu.VMEM)],
        out_specs=pl.BlockSpec(memory_space=pl.ANY),
        scratch_shapes=[dma] + stage,
        compiler_params=pltpu.CompilerParams(collective_id=0, has_side_effects=True),
        name="gather_all",
    )(block)


def reduce_kernel(
    sizes, p_ref, o_ref, acc, sib, r1, r2, r3, s_send, s_recv, c1_send, c1_recv, c2_send, c2_recv, c3_send, c3_recv
):
    me = Place(sizes)
    nz, nx, ny = sizes
    z, x, y, c = me.z, me.x, me.y, me.c
    width = o_ref.shape[1]
    cols = halves_of(width)
    whole = (pl.ds(0, width),)
    me.greet()
    started = []

    def remote(src, dst, ssem, rsem, dev):
        return pltpu.make_async_remote_copy(
            src_ref=src, dst_ref=dst, send_sem=ssem, recv_sem=rsem, device_id=dev, device_id_type=MESH
        )

    def part(by, core):
        return pl.ds(pl.multiple_of((by * CORES + core) * width, LANES), width)

    blocks = [(bz, bx, by) for bz in range(nz) for bx in range(nx) for by in range(ny)]
    for bz, bx, by in blocks:
        a = bz * nx + bx
        copy = remote(
            p_ref.at[a, :, part(by, 1 - c)], sib.at[a, by], s_send.at[a, by], s_recv.at[a, by], me.device(c=1 - c)
        )
        copy.start()
        started.append((None, copy))

    def add(view, col, from_ref):
        view[:, col] = (view[:, col].astype(jnp.float32) + from_ref[:, col].astype(jnp.float32)).astype(view.dtype)

    def receive(view, col, landing, way, ssem, rsem):
        remote(landing[way].at[:, col], landing[way].at[:, col], ssem.at[way], rsem.at[way], me.device(c=1 - c)).wait_recv()
        add(view, col, landing[way])

    def chain(view, col, name, target, landing, ssem, rsem, here=None):
        p, n = {"x": (x, nx), "y": (y, ny), "z": (z, nz)}[name]
        for way in range(2):
            to = p + 1 if way == 0 else p - 1
            go = p < target if way == 0 else p > target
            if here is not None:
                go = jnp.logical_and(here, go)
            inner = p > 0 if way == 0 else p < n - 1
            if n > 2:
                pl.when(jnp.logical_and(go, inner))(
                    functools.partial(receive, view, col, landing, way, ssem, rsem)
                )
            copy = remote(
                view.at[:, col], landing[way].at[:, col], ssem.at[way], rsem.at[way], me.device(**{name: to})
            )
            pl.when(go)(copy.start)
            started.append((go, copy))

    def finish(here, view, col, name, landing, ssem, rsem):
        p, n = {"x": (x, nx), "y": (y, ny), "z": (z, nz)}[name]
        for way in range(2):
            cond = p > 0 if way == 0 else p < n - 1
            cond = jnp.logical_and(here, cond)
            pl.when(cond)(functools.partial(receive, view, col, landing, way, ssem, rsem))

    def lines(h, bx, by):
        first, last = (("y", by), ("x", bx)) if h == 0 else (("x", bx), ("y", by))
        return first, last

    def first_args(h, a, by):
        return [r1.at[way, a, by] for way in range(2)], c1_send.at[h, a, by], c1_recv.at[h, a, by]

    def second_args(h, bz, bx, by):
        k = bz * max(nx, ny) + (bx if h == 0 else by)
        return [r2.at[way, k] for way in range(2)], c2_send.at[h, k], c2_recv.at[h, k]

    at = {"x": x, "y": y}
    for bz, bx, by in blocks:
        a = bz * nx + bx
        remote(sib.at[a, by], sib.at[a, by], s_send.at[a, by], s_recv.at[a, by], me.device(c=1 - c)).wait_recv()
        acc[a, by] = (
            p_ref[a, :, part(by, c)].astype(jnp.float32) + sib[a, by].astype(jnp.float32)
        ).astype(acc.dtype)
        for h in range(2):
            (name, target), _ = lines(h, bx, by)
            chain(acc.at[a, by], cols[h], name, target, *first_args(h, a, by))
    for bz, bx, by in blocks:
        a = bz * nx + bx
        for h in range(2):
            (name, target), (name2, target2) = lines(h, bx, by)
            here = at[name] == target
            finish(here, acc.at[a, by], cols[h], name, *first_args(h, a, by))
            chain(acc.at[a, by], cols[h], name2, target2, *second_args(h, bz, bx, by), here=here)
    for bz, bx, by in blocks:
        a = bz * nx + bx
        here = jnp.logical_and(x == bx, y == by)
        for h in range(2):
            _, (name2, target2) = lines(h, bx, by)
            finish(here, acc.at[a, by], cols[h], name2, *second_args(h, bz, bx, by))
    for bz in sorted(range(nz), key=lambda place: min(place, nz - 1 - place)):
        view = acc.at[bz * nx + x, y]
        landing = [r3.at[way, bz] for way in range(2)]
        chain(view, whole[0], "z", bz, landing, c3_send.at[bz], c3_recv.at[bz])
    for bz in range(nz):
        landing = [r3.at[way, bz] for way in range(2)]

        @pl.when(z == bz)
        def _():
            total = acc[bz * nx + x, y].astype(jnp.float32)
            o_ref[...] = total

        for way in range(2):
            cond = jnp.logical_and(z == bz, z > 0 if way == 0 else z < nz - 1)

            @pl.when(cond)
            def _():
                remote(
                    landing[way], landing[way], c3_send.at[bz, way], c3_recv.at[bz, way], me.device(c=1 - c)
                ).wait_recv()
                o_ref[...] += landing[way][...].astype(jnp.float32)

    for cond, copy in started:
        if cond is None:
            copy.wait_send()
        else:
            pl.when(cond)(copy.wait_send)


def reduce_all(partial, sizes):
    nz, nx, ny = sizes
    attn, rows, full = partial.shape
    width = full // (ny * CORES)
    wide = max(nx, ny)
    dma = pltpu.SemaphoreType.DMA
    kind = partial.dtype
    return pl.pallas_call(
        functools.partial(reduce_kernel, sizes),
        out_shape=jax.ShapeDtypeStruct((rows, width), jnp.float32),
        in_specs=[pl.BlockSpec(memory_space=pltpu.VMEM)],
        out_specs=pl.BlockSpec(memory_space=pltpu.VMEM),
        scratch_shapes=[
            pltpu.VMEM((attn, ny, rows, width), kind),
            pltpu.VMEM((attn, ny, rows, width), kind),
            pltpu.VMEM((2, attn, ny, rows, width), kind),
            pltpu.VMEM((2, nz * wide, rows, width), kind),
            pltpu.VMEM((2, nz, rows, width), kind),
        ]
        + [dma((attn, ny))] * 2
        + [dma((2, attn, ny, 2))] * 2
        + [dma((2, nz * wide, 2))] * 2
        + [dma((nz, 2))] * 2,
        compiler_params=pltpu.CompilerParams(
            collective_id=1, has_side_effects=True, vmem_limit_bytes=60 * 2**20
        ),
        name="reduce_all",
    )(partial)


def pick_kernel(sel_ref, g_ref, out_ref):
    local, cap, rows = sel_ref.shape[1:]
    devices = g_ref.shape[1]
    width = out_ref.shape[2] // devices
    chosen = sel_ref[0].reshape(local * cap, rows)
    for e in range(devices):
        taken = jnp.dot(chosen, g_ref[0, e, :, :width], preferred_element_type=jnp.float32)
        taken = taken.astype(out_ref.dtype).reshape(local, cap, width)
        out_ref[:, :, e * width : (e + 1) * width] = taken


def pick_rows(selector, gathered, width):
    attn, local, cap, rows = selector.shape
    devices, full = gathered.shape[1], gathered.shape[3]
    return pl.pallas_call(
        pick_kernel,
        grid=(attn,),
        out_shape=jax.ShapeDtypeStruct((local, attn * cap, devices * width), gathered.dtype),
        in_specs=[
            pl.BlockSpec((1, local, cap, rows), lambda a: (a, 0, 0, 0)),
            pl.BlockSpec((1, devices, rows, full), lambda a: (a, 0, 0, 0)),
        ],
        out_specs=pl.BlockSpec((local, cap, devices * width), lambda a: (0, a, 0)),
        name="pick_rows",
    )(selector, gathered)


def place_kernel(sel_ref, y_ref, out_ref):
    local = sel_ref.shape[1]
    total = None
    for n in range(local):
        term = lax.dot_general(
            sel_ref[0, n], y_ref[n], (((0,), (0,)), ((), ())), preferred_element_type=jnp.float32
        )
        total = term if total is None else total + term
    out_ref[0] = total.astype(out_ref.dtype)


def place_rows(selector, outputs):
    attn, local, cap, rows = selector.shape
    full = outputs.shape[2]
    return pl.pallas_call(
        place_kernel,
        grid=(attn,),
        out_shape=jax.ShapeDtypeStruct((attn, rows, full), jnp.bfloat16),
        in_specs=[
            pl.BlockSpec((1, local, cap, rows), lambda a: (a, 0, 0, 0)),
            pl.BlockSpec((local, cap, full), lambda a: (0, a, 0)),
        ],
        out_specs=pl.BlockSpec((1, rows, full), lambda a: (a, 0, 0)),
        name="place_rows",
    )(selector, outputs)


def on_device(
    sizes,
    resid,
    query,
    key_cache,
    value_cache,
    new_key,
    new_value,
    lengths,
    norm_gain,
    router_weight,
    expert_ids,
    w_gate,
    w_up,
    w_down,
):
    row_count, width_local = resid.shape
    kv_local, cache_slots, head_size = key_cache.shape[1:]
    group_size = query.shape[1] // (kv_local * head_size)
    local_experts, features, _ = w_gate.shape
    experts = router_weight.shape[1]
    cap = row_count // 2
    score_scale = 1.0 / math.sqrt(head_size)
    queries = query.reshape(row_count, kv_local, group_size, head_size)
    scores = (
        jnp.einsum("rkgd,rkld->rkgl", queries, key_cache, preferred_element_type=jnp.float32) * score_scale
    )
    fresh_score = (
        jnp.einsum(
            "rkgd,rkd->rkg",
            queries,
            new_key.reshape(row_count, kv_local, head_size),
            preferred_element_type=jnp.float32,
        )
        * score_scale
    )
    usable = lax.broadcasted_iota(jnp.int32, (row_count, cache_slots), 1) < lengths[:, None]
    powers = jnp.where(usable[:, None, None, :], jnp.exp(scores), jnp.float32(0.0))
    fresh_power = jnp.exp(fresh_score)
    denominator = jnp.sum(powers, axis=-1) + fresh_power
    weights_cache = (powers / denominator[..., None]).astype(jnp.bfloat16)
    weight_fresh = (fresh_power / denominator).astype(jnp.bfloat16)
    attended = jnp.einsum(
        "rkgl,rkld->rkgd", weights_cache, value_cache, preferred_element_type=jnp.float32
    )
    attended = attended + weight_fresh.astype(jnp.float32)[..., None] * new_value.astype(
        jnp.float32
    ).reshape(row_count, kv_local, 1, head_size)
    hidden_state = resid.astype(jnp.float32) + attended.reshape(row_count, width_local)
    gained = hidden_state * norm_gain
    square = jnp.sum(hidden_state * hidden_state, axis=1, keepdims=True)
    raw_logits = jnp.dot(gained, router_weight, precision=lax.Precision.HIGHEST)
    stats = jnp.concatenate([raw_logits, square], axis=1)
    pieces, rest = [], jnp.pad(stats, ((0, 0), (0, STAT - experts - 1)))
    for _ in range(PARTS):
        piece = lax.reduce_precision(rest, 8, 7)
        pieces.append(piece)
        rest = rest - piece
    pieces.append(expert_ids.astype(jnp.float32))
    packed = jnp.concatenate(pieces, axis=1)
    packed = jnp.pad(packed, ((0, 0), (0, LANES - packed.shape[1])))
    block = jnp.concatenate([gained, packed], axis=1).astype(jnp.bfloat16)

    gathered = gather_all(block, sizes)
    attn = gathered.shape[0]

    tail = gathered[:, :, :, width_local:].astype(jnp.float32)
    summed = jnp.sum(tail[..., : PARTS * STAT], axis=1)
    summed = sum(summed[..., k * STAT : (k + 1) * STAT] for k in range(PARTS))
    scale = lax.rsqrt(summed[..., experts] / features + EPSILON)
    logits = summed[..., :experts] * scale[..., None]
    ids = tail[:, 0, :, PARTS * STAT : PARTS * STAT + 2].astype(jnp.int32)
    choose = ids[..., None] == lax.broadcasted_iota(jnp.int32, (1, 1, 1, experts), 3)
    picked = jnp.sum(jnp.where(choose, logits[:, :, None, :], jnp.float32(0.0)), axis=3)
    first_weight = 1.0 / (1.0 + jnp.exp(picked[..., 1] - picked[..., 0]))
    second_weight = 1.0 / (1.0 + jnp.exp(picked[..., 0] - picked[..., 1]))
    own = lax.axis_index("expert") * local_experts + jnp.arange(local_experts, dtype=jnp.int32)
    mine = ids[:, None, :, :] == own[None, :, None, None]
    hit = jnp.any(mine, axis=3)
    earlier = jnp.tril(jnp.ones((row_count, row_count), jnp.bfloat16), -1)
    before = jnp.einsum(
        "anr,qr->anq", hit.astype(jnp.bfloat16), earlier, preferred_element_type=jnp.float32
    ).astype(jnp.int32)
    match = jnp.logical_and(
        hit[:, :, None, :], before[:, :, None, :] == lax.broadcasted_iota(jnp.int32, (1, 1, cap, 1), 2)
    )
    selector = match.astype(jnp.bfloat16)
    row_weight = jnp.where(mine[..., 0], first_weight[:, None, :], jnp.float32(0.0)) + jnp.where(
        mine[..., 1], second_weight[:, None, :], jnp.float32(0.0)
    )

    def per_slot(values):
        out = jnp.sum(jnp.where(match, values[:, :, None, :], jnp.float32(0.0)), axis=3)
        return jnp.swapaxes(out, 0, 1).reshape(local_experts, attn * cap, 1)

    slot_weight = per_slot(row_weight)
    slot_scale = per_slot(jnp.broadcast_to(scale[:, None, :], row_weight.shape))

    slab_rows = pick_rows(selector, gathered, width_local)
    gate_part = jnp.einsum("end,edf->enf", slab_rows, w_gate, preferred_element_type=jnp.float32) * slot_scale
    up_part = jnp.einsum("end,edf->enf", slab_rows, w_up, preferred_element_type=jnp.float32) * slot_scale
    activation = (jax.nn.silu(gate_part) * up_part * slot_weight).astype(jnp.bfloat16)
    outputs = jnp.einsum("enf,efd->end", activation, w_down, preferred_element_type=jnp.float32).astype(
        jnp.bfloat16
    )
    partial = place_rows(selector, outputs)
    total = reduce_all(partial, sizes)
    return (hidden_state + total).astype(jnp.bfloat16)


def solution(mesh):
    sizes = grid_of(mesh.shape["attn"], mesh.shape["expert"])
    return jax.shard_map(
        functools.partial(on_device, sizes),
        mesh=mesh,
        in_specs=(
            P("attn", "expert"),
            P("attn", "expert"),
            P("attn", "expert", None, None),
            P("attn", "expert", None, None),
            P("attn", "expert"),
            P("attn", "expert"),
            P("attn"),
            P("expert"),
            P("expert", None),
            P("attn", None),
            P("expert", None, "attn"),
            P("expert", None, "attn"),
            P("expert", "attn", None),
        ),
        out_specs=P("attn", "expert"),
        check_vma=False,
    )
```

```python
import functools
import math

import jax
import jax.numpy as jnp
from jax import lax
from jax.experimental import pallas as pl
from jax.experimental.pallas import tpu as pltpu
from jax.sharding import PartitionSpec as P

EPSILON = 1e-05
LANES = 128
CORES = 2
PARTS = 3
STAT = 16
TILE = 256
MESH = pl.DeviceIdType.MESH


def grid_of(attn, expert):
    ny = max(expert // CORES, 1)
    nx = ny if attn % ny == 0 else 1
    return attn // nx, nx, ny


def halves_of(width):
    tiles = width // LANES
    first = (tiles - tiles // 2) * LANES
    return pl.ds(0, first), pl.ds(first, width - first)


class Place:
    def __init__(self, sizes):
        self.nz, self.nx, self.ny = sizes
        a = lax.axis_index("attn")
        e = lax.axis_index("expert")
        self.z, self.x = a // self.nx, lax.rem(a, self.nx)
        self.y, self.c = e // CORES, lax.rem(e, CORES)

    def device(self, z=None, x=None, y=None, c=None):
        z = self.z if z is None else z
        x = self.x if x is None else x
        y = self.y if y is None else y
        c = self.c if c is None else c
        return (z * self.nx + x, y * CORES + c)

    def greet(self):
        barrier = pltpu.get_barrier_semaphore()
        count = jnp.int32(1)

        def signal(dev):
            pl.semaphore_signal(barrier, inc=1, device_id=dev, device_id_type=MESH)

        signal(self.device(c=1 - self.c))
        for name, p, n in (("z", self.z, self.nz), ("x", self.x, self.nx), ("y", self.y, self.ny)):
            for step in (-1, 1):
                inside = jnp.logical_and(p + step >= 0, p + step < n)
                pl.when(inside)(functools.partial(signal, self.device(**{name: p + step})))
                count = count + inside.astype(jnp.int32)
        pl.semaphore_wait(barrier, count)


def gather_kernel(sizes, x_ref, g_ref, local_sem, z_send, z_recv, p1_send, p1_recv, p2_send, p2_recv, s_send, s_recv):
    me = Place(sizes)
    nz, nx, ny = sizes
    z, x, y, c = me.z, me.x, me.y, me.c
    width = x_ref.shape[1]
    cols = halves_of(width)
    me.greet()
    started = []

    def send(cond, src, dst, ssem, rsem, dev):
        copy = pltpu.make_async_remote_copy(
            src_ref=src, dst_ref=dst, send_sem=ssem, recv_sem=rsem, device_id=dev, device_id_type=MESH
        )
        started.append((cond, copy))
        if cond is None:
            copy.start()
        else:
            pl.when(cond)(copy.start)

    def await_block(dst, ssem, rsem):
        pltpu.make_async_remote_copy(
            src_ref=dst, dst_ref=dst, send_sem=ssem, recv_sem=rsem,
            device_id=me.device(c=1 - c), device_id_type=MESH,
        ).wait_recv()

    def block(bz, bx, by, core=None):
        core = c if core is None else core
        return g_ref.at[bz * nx + bx, by * CORES + core]

    def half(ref, h):
        return ref.at[:, cols[h]]

    def to_sibling(cond, src, bz, bx, by, h):
        slot = (bz * nx + bx, by, h)
        send(cond, half(src, h), half(block(bz, bx, by), h), s_send.at[slot], s_recv.at[slot], me.device(c=1 - c))

    def line(h, stage):
        return ("x", x, nx) if (h == 0) == (stage == 0) else ("y", y, ny)

    def along(cond, src, dst, h, stage, step, way, slot):
        name, p, n = line(h, stage)
        to = p + 1 if way == 0 else p - 1
        inside = to < n if way == 0 else to >= 0
        ssem, rsem = (p1_send, p1_recv) if stage == 0 else (p2_send, p2_recv)
        index = (h, step, way) + slot
        cond = inside if cond is None else jnp.logical_and(cond, inside)
        send(cond, half(src, h), half(dst, h), ssem.at[index], rsem.at[index], me.device(**{name: to}))

    def spread(cond, src, bz):
        for h in range(2):
            for way in range(2):
                along(cond, src, block(bz, x, y), h, 0, 0, way, (bz,))
            to_sibling(cond, src, bz, x, y, h)

    def z_hop(cond, src, bz, step, way):
        to = z + 1 if way == 0 else z - 1
        inside = to < nz if way == 0 else to >= 0
        cond = inside if cond is None else jnp.logical_and(cond, inside)
        send(cond, src, block(bz, x, y), z_send.at[step, way], z_recv.at[step, way], me.device(z=to))

    def second(cond, src, dst, h, bz, other):
        for way in range(2):
            along(cond, src, dst, h, 1, 0, way, (bz, other))

    def places(step):
        if step == 0:
            return [(None, z)]
        return [(z - step >= 0, z - step), (z + step < nz, z + step)]

    def both(one, two):
        return two if one is None else jnp.logical_and(one, two)

    def first_arrivals(distance):
        for step in range(1, max(nx, ny)):
            for there, bz in places(distance):
                for h in range(2):
                    name, p, n = line(h, 0)
                    if step >= n:
                        continue
                    for way in range(2):
                        q = p - step if way == 0 else p + step
                        have = both(there, q >= 0 if way == 0 else q < n)
                        bx, by = (q, y) if name == "x" else (x, q)
                        dst = block(bz, bx, by)
                        index = (h, step - 1, way, bz)
                        pl.when(have)(
                            functools.partial(await_block, half(dst, h), p1_send.at[index], p1_recv.at[index])
                        )
                        if step < n - 1:
                            along(have, dst, dst, h, 0, step, way, (bz,))
                        second(have, dst, dst, h, bz, q)
                        to_sibling(have, dst, bz, bx, by, h)

    def second_arrivals(distance):
        for step in range(1, max(nx, ny)):
            for k in range(max(nx, ny)):
                for there, bz in places(distance):
                    for h in range(2):
                        _, first_p, first_n = line(h, 0)
                        name, p, n = line(h, 1)
                        if step >= n or k >= first_n:
                            continue
                        other = lax.rem(first_p + k, first_n)
                        for way in range(2):
                            q = p - step if way == 0 else p + step
                            have = both(there, q >= 0 if way == 0 else q < n)
                            bx, by = (q, other) if name == "x" else (other, q)
                            dst = block(bz, bx, by)
                            index = (h, step - 1, way, bz, other)
                            pl.when(have)(
                                functools.partial(await_block, half(dst, h), p2_send.at[index], p2_recv.at[index])
                            )
                            if step < n - 1:
                                along(have, dst, dst, h, 1, step, way, (bz, other))
                            to_sibling(have, dst, bz, bx, by, h)

    for way in range(2):
        if nz > 1:
            z_hop(None, x_ref, z, 0, way)
    spread(None, x_ref, z)
    for h in range(2):
        second(None, x_ref, block(z, x, y), h, z, line(h, 0)[1])
    local = pltpu.make_async_copy(x_ref, block(z, x, y), local_sem)
    local.start()
    for step in range(1, nz + 2):
        if step < nz:
            for way, (have, bz) in enumerate(places(step)):
                dst = block(bz, x, y)
                pl.when(have)(functools.partial(await_block, dst, z_send.at[step - 1, way], z_recv.at[step - 1, way]))
                if step < nz - 1:
                    z_hop(have, dst, bz, step, way)
                spread(have, dst, bz)
                for h in range(2):
                    second(have, dst, dst, h, bz, line(h, 0)[1])
        if step <= nz:
            first_arrivals(step - 1)
        if step >= 2:
            second_arrivals(step - 2)
    local.wait()
    for bz in range(nz):
        for bx in range(nx):
            for by in range(ny):
                for h in range(2):
                    slot = (bz * nx + bx, by, h)
                    await_block(half(block(bz, bx, by, 1 - c), h), s_send.at[slot], s_recv.at[slot])
    for cond, copy in started:
        if cond is None:
            copy.wait_send()
        else:
            pl.when(cond)(copy.wait_send)


def gather_all(block, sizes):
    nz, nx, ny = sizes
    rows, width = block.shape
    wide = max(nx, ny)
    steps = max(wide - 1, 1)
    dma = pltpu.SemaphoreType.DMA
    stage = [dma((max(nz - 1, 1), 2))] * 2 + [dma((2, steps, 2, nz))] * 2
    stage += [dma((2, steps, 2, nz, wide))] * 2 + [dma((nz * nx, ny, 2))] * 2
    return pl.pallas_call(
        functools.partial(gather_kernel, sizes),
        out_shape=jax.ShapeDtypeStruct((nz * nx, ny * CORES, rows, width), block.dtype),
        in_specs=[pl.BlockSpec(memory_space=pltpu.VMEM)],
        out_specs=pl.BlockSpec(memory_space=pl.ANY),
        scratch_shapes=[dma] + stage,
        compiler_params=pltpu.CompilerParams(collective_id=0, has_side_effects=True),
        name="gather_all",
    )(block)


def reduce_kernel(
    sizes,
    act_ref,
    sel_ref,
    w_ref,
    o_ref,
    p_ref,
    w_buf,
    acc,
    sib,
    r1,
    r2,
    r3,
    w_sem,
    s_send,
    s_recv,
    c1_send,
    c1_recv,
    c2_send,
    c2_recv,
    c3_send,
    c3_recv,
):
    me = Place(sizes)
    nz, nx, ny = sizes
    z, x, y, c = me.z, me.x, me.y, me.c
    width = o_ref.shape[1]
    cols = halves_of(width)
    whole = (pl.ds(0, width),)
    local = act_ref.shape[0]
    groups, group_rows, deep = sel_ref.shape
    slots = deep // local
    per_group = group_rows // p_ref.shape[1]
    tile = math.gcd(width, TILE)
    started = []

    def remote(src, dst, ssem, rsem, dev):
        return pltpu.make_async_remote_copy(
            src_ref=src, dst_ref=dst, send_sem=ssem, recv_sem=rsem, device_id=dev, device_id_type=MESH
        )

    def part(by, core):
        return pl.ds(pl.multiple_of((by * CORES + core) * width, LANES), width)

    chunks = [(by, core) for core in (1 - c, c) for by in range(ny)]
    loads = []
    for k, (by, core) in enumerate(chunks):
        load = pltpu.make_async_copy(w_ref.at[:, :, part(by, core)], w_buf.at[k], w_sem.at[k])
        load.start()
        loads.append(load)
    me.greet()

    def project(k, by, core):
        base = (by * CORES + core) * width

        def one(t, carry):
            offset = pl.multiple_of(t * tile, tile)
            place = pl.ds(pl.multiple_of(base + offset, LANES), tile)
            outs = [
                jnp.dot(
                    act_ref[n], w_buf[k, n, :, pl.ds(offset, tile)], preferred_element_type=jnp.float32
                ).astype(p_ref.dtype)
                for n in range(local)
            ]
            for g in range(groups):
                mixed = [out[g * slots : (g + 1) * slots] for out in outs]
                mixed = mixed[0] if local == 1 else jnp.concatenate(mixed, axis=0)
                rows = jnp.dot(sel_ref[g], mixed, preferred_element_type=jnp.float32).astype(p_ref.dtype)
                for i in range(per_group):
                    p_ref[g * per_group + i, :, place] = rows[i * p_ref.shape[1] : (i + 1) * p_ref.shape[1]]
            return carry

        lax.fori_loop(0, width // tile, one, 0)

    for k, (by, core) in enumerate(chunks):
        loads[k].wait()
        project(k, by, core)
        if k < ny:
            for a in range(nz * nx):
                copy = remote(
                    p_ref.at[a, :, part(by, 1 - c)], sib.at[a, by], s_send.at[a, by], s_recv.at[a, by],
                    me.device(c=1 - c),
                )
                copy.start()
                started.append((None, copy))

    def add(view, col, from_ref):
        view[:, col] = (view[:, col].astype(jnp.float32) + from_ref[:, col].astype(jnp.float32)).astype(view.dtype)

    def receive(view, col, landing, way, ssem, rsem):
        remote(landing[way].at[:, col], landing[way].at[:, col], ssem.at[way], rsem.at[way], me.device(c=1 - c)).wait_recv()
        add(view, col, landing[way])

    def chain(view, col, name, target, landing, ssem, rsem, here=None):
        p, n = {"x": (x, nx), "y": (y, ny), "z": (z, nz)}[name]
        for way in range(2):
            to = p + 1 if way == 0 else p - 1
            go = p < target if way == 0 else p > target
            if here is not None:
                go = jnp.logical_and(here, go)
            inner = p > 0 if way == 0 else p < n - 1
            if n > 2:
                pl.when(jnp.logical_and(go, inner))(
                    functools.partial(receive, view, col, landing, way, ssem, rsem)
                )
            copy = remote(
                view.at[:, col], landing[way].at[:, col], ssem.at[way], rsem.at[way], me.device(**{name: to})
            )
            pl.when(go)(copy.start)
            started.append((go, copy))

    def finish(here, view, col, name, landing, ssem, rsem):
        p, n = {"x": (x, nx), "y": (y, ny), "z": (z, nz)}[name]
        for way in range(2):
            cond = p > 0 if way == 0 else p < n - 1
            cond = jnp.logical_and(here, cond)
            pl.when(cond)(functools.partial(receive, view, col, landing, way, ssem, rsem))

    def lines(h, bx, by):
        first, last = (("y", by), ("x", bx)) if h == 0 else (("x", bx), ("y", by))
        return first, last

    def first_args(h, a, by):
        return [r1.at[way, a, by] for way in range(2)], c1_send.at[h, a, by], c1_recv.at[h, a, by]

    def second_args(h, bz, bx, by):
        k = bz * max(nx, ny) + (bx if h == 0 else by)
        return [r2.at[way, k] for way in range(2)], c2_send.at[h, k], c2_recv.at[h, k]

    at = {"x": x, "y": y}
    plane = [(bx, by) for bx in range(nx) for by in range(ny)]

    def begin(bz):
        for bx, by in plane:
            a = bz * nx + bx
            remote(sib.at[a, by], sib.at[a, by], s_send.at[a, by], s_recv.at[a, by], me.device(c=1 - c)).wait_recv()
            acc[a, by] = (
                p_ref[a, :, part(by, c)].astype(jnp.float32) + sib[a, by].astype(jnp.float32)
            ).astype(acc.dtype)
            for h in range(2):
                (name, target), _ = lines(h, bx, by)
                chain(acc.at[a, by], cols[h], name, target, *first_args(h, a, by))

    def go_on(bz):
        for bx, by in plane:
            a = bz * nx + bx
            for h in range(2):
                (name, target), (name2, target2) = lines(h, bx, by)
                here = at[name] == target
                finish(here, acc.at[a, by], cols[h], name, *first_args(h, a, by))
                chain(acc.at[a, by], cols[h], name2, target2, *second_args(h, bz, bx, by), here=here)

    def to_z(bz):
        for bx, by in plane:
            here = jnp.logical_and(x == bx, y == by)
            for h in range(2):
                _, (name2, _) = lines(h, bx, by)
                finish(here, acc.at[bz * nx + bx, by], cols[h], name2, *second_args(h, bz, bx, by))
        landing = [r3.at[way, bz] for way in range(2)]
        chain(acc.at[bz * nx + x, y], whole[0], "z", bz, landing, c3_send.at[bz], c3_recv.at[bz])

    order = sorted(range(nz), key=lambda place: min(place, nz - 1 - place))
    for k in range(nz + 2):
        if k < nz:
            begin(order[k])
        if 1 <= k <= nz:
            go_on(order[k - 1])
        if k >= 2:
            to_z(order[k - 2])
    for bz in range(nz):
        landing = [r3.at[way, bz] for way in range(2)]

        @pl.when(z == bz)
        def _():
            total = acc[bz * nx + x, y].astype(jnp.float32)
            o_ref[...] = total

        for way in range(2):
            cond = jnp.logical_and(z == bz, z > 0 if way == 0 else z < nz - 1)

            @pl.when(cond)
            def _():
                remote(
                    landing[way], landing[way], c3_send.at[bz, way], c3_recv.at[bz, way], me.device(c=1 - c)
                ).wait_recv()
                o_ref[...] += landing[way][...].astype(jnp.float32)

    for cond, copy in started:
        if cond is None:
            copy.wait_send()
        else:
            pl.when(cond)(copy.wait_send)


def reduce_all(activation, selector, w_down, sizes):
    nz, nx, ny = sizes
    local, depth, full = w_down.shape
    attn = nz * nx
    rows = selector.shape[0] * selector.shape[1] // attn
    width = full // (ny * CORES)
    wide = max(nx, ny)
    dma = pltpu.SemaphoreType.DMA
    kind = activation.dtype
    return pl.pallas_call(
        functools.partial(reduce_kernel, sizes),
        out_shape=jax.ShapeDtypeStruct((rows, width), jnp.float32),
        in_specs=[pl.BlockSpec(memory_space=pltpu.VMEM)] * 2 + [pl.BlockSpec(memory_space=pl.ANY)],
        out_specs=pl.BlockSpec(memory_space=pltpu.VMEM),
        scratch_shapes=[
            pltpu.VMEM((attn, rows, full), kind),
            pltpu.VMEM((ny * CORES, local, depth, width), kind),
            pltpu.VMEM((attn, ny, rows, width), kind),
            pltpu.VMEM((attn, ny, rows, width), kind),
            pltpu.VMEM((2, attn, ny, rows, width), kind),
            pltpu.VMEM((2, nz * wide, rows, width), kind),
            pltpu.VMEM((2, nz, rows, width), kind),
            dma((ny * CORES,)),
        ]
        + [dma((attn, ny))] * 2
        + [dma((2, attn, ny, 2))] * 2
        + [dma((2, nz * wide, 2))] * 2
        + [dma((nz, 2))] * 2,
        compiler_params=pltpu.CompilerParams(
            collective_id=1, has_side_effects=True, vmem_limit_bytes=60 * 2**20
        ),
        name="reduce_all",
    )(activation, selector, w_down)


def pick_kernel(sel_ref, g_ref, out_ref):
    local, slots, width = out_ref.shape
    rows = sel_ref.shape[1]
    taken = lax.dot_general(
        sel_ref[0],
        g_ref[:, 0, :, :width].reshape(rows, width),
        (((0,), (0,)), ((), ())),
        preferred_element_type=jnp.float32,
    )
    out_ref[...] = taken.astype(out_ref.dtype).reshape(local, slots, width)


def pick_rows(selector, gathered, width, local):
    groups, group_rows, deep = selector.shape
    attn, devices, rows, full = gathered.shape
    per_group = attn // groups
    slots = deep // local
    return pl.pallas_call(
        pick_kernel,
        grid=(groups, devices),
        out_shape=jax.ShapeDtypeStruct((local, groups * slots, devices * width), gathered.dtype),
        in_specs=[
            pl.BlockSpec((1, group_rows, deep), lambda g, e: (g, 0, 0)),
            pl.BlockSpec((per_group, 1, rows, full), lambda g, e: (g, e, 0, 0)),
        ],
        out_specs=pl.BlockSpec((local, slots, width), lambda g, e: (0, g, e)),
        name="pick_rows",
    )(selector, gathered)


def on_device(
    sizes,
    resid,
    query,
    key_cache,
    value_cache,
    new_key,
    new_value,
    lengths,
    norm_gain,
    router_weight,
    expert_ids,
    w_gate,
    w_up,
    w_down,
):
    row_count, width_local = resid.shape
    kv_local, cache_slots, head_size = key_cache.shape[1:]
    group_size = query.shape[1] // (kv_local * head_size)
    local_experts, features, _ = w_gate.shape
    experts = router_weight.shape[1]
    cap = row_count // 2
    score_scale = 1.0 / math.sqrt(head_size)
    queries = query.reshape(row_count, kv_local, group_size, head_size)
    scores = (
        jnp.einsum("rkgd,rkld->rkgl", queries, key_cache, preferred_element_type=jnp.float32) * score_scale
    )
    fresh_score = (
        jnp.einsum(
            "rkgd,rkd->rkg",
            queries,
            new_key.reshape(row_count, kv_local, head_size),
            preferred_element_type=jnp.float32,
        )
        * score_scale
    )
    usable = lax.broadcasted_iota(jnp.int32, (row_count, cache_slots), 1) < lengths[:, None]
    powers = jnp.where(usable[:, None, None, :], jnp.exp(scores), jnp.float32(0.0))
    fresh_power = jnp.exp(fresh_score)
    denominator = jnp.sum(powers, axis=-1) + fresh_power
    weights_cache = (powers / denominator[..., None]).astype(jnp.bfloat16)
    weight_fresh = (fresh_power / denominator).astype(jnp.bfloat16)
    attended = jnp.einsum(
        "rkgl,rkld->rkgd", weights_cache, value_cache, preferred_element_type=jnp.float32
    )
    attended = attended + weight_fresh.astype(jnp.float32)[..., None] * new_value.astype(
        jnp.float32
    ).reshape(row_count, kv_local, 1, head_size)
    hidden_state = resid.astype(jnp.float32) + attended.reshape(row_count, width_local)
    gained = hidden_state * norm_gain
    square = jnp.sum(hidden_state * hidden_state, axis=1, keepdims=True)
    raw_logits = jnp.dot(gained, router_weight, precision=lax.Precision.HIGHEST)
    stats = jnp.concatenate([raw_logits, square], axis=1)
    pieces, rest = [], jnp.pad(stats, ((0, 0), (0, STAT - experts - 1)))
    for _ in range(PARTS):
        piece = lax.reduce_precision(rest, 8, 7)
        pieces.append(piece)
        rest = rest - piece
    pieces.append(expert_ids.astype(jnp.float32))
    packed = jnp.concatenate(pieces, axis=1)
    packed = jnp.pad(packed, ((0, 0), (0, LANES - packed.shape[1])))
    block = jnp.concatenate([gained, packed], axis=1).astype(jnp.bfloat16)

    gathered = gather_all(block, sizes)
    attn = gathered.shape[0]

    tail = gathered[:, :, :, width_local:].astype(jnp.float32)
    summed = jnp.sum(tail[..., : PARTS * STAT], axis=1)
    summed = sum(summed[..., k * STAT : (k + 1) * STAT] for k in range(PARTS))
    scale = lax.rsqrt(summed[..., experts] / features + EPSILON)
    logits = summed[..., :experts] * scale[..., None]
    ids = tail[:, 0, :, PARTS * STAT : PARTS * STAT + 2].astype(jnp.int32)
    choose = ids[..., None] == lax.broadcasted_iota(jnp.int32, (1, 1, 1, experts), 3)
    picked = jnp.sum(jnp.where(choose, logits[:, :, None, :], jnp.float32(0.0)), axis=3)
    first_weight = 1.0 / (1.0 + jnp.exp(picked[..., 1] - picked[..., 0]))
    second_weight = 1.0 / (1.0 + jnp.exp(picked[..., 0] - picked[..., 1]))
    own = lax.axis_index("expert") * local_experts + jnp.arange(local_experts, dtype=jnp.int32)
    mine = ids[:, None, :, :] == own[None, :, None, None]
    hit = jnp.any(mine, axis=3)
    earlier = jnp.tril(jnp.ones((row_count, row_count), jnp.bfloat16), -1)
    before = jnp.einsum(
        "anr,qr->anq", hit.astype(jnp.bfloat16), earlier, preferred_element_type=jnp.float32
    ).astype(jnp.int32)
    match = jnp.logical_and(
        hit[:, :, None, :], before[:, :, None, :] == lax.broadcasted_iota(jnp.int32, (1, 1, cap, 1), 2)
    )
    per_group = math.gcd(attn, max(TILE // row_count, 1))
    split = match.reshape(attn // per_group, per_group, local_experts, cap, row_count)
    same = jnp.eye(per_group, dtype=bool)
    selector = jnp.logical_and(
        jnp.transpose(split, (0, 1, 4, 2, 3))[:, :, :, :, None, :], same[None, :, None, None, :, None]
    )
    selector = selector.reshape(attn // per_group, per_group * row_count, -1).astype(jnp.bfloat16)
    row_weight = jnp.where(mine[..., 0], first_weight[:, None, :], jnp.float32(0.0)) + jnp.where(
        mine[..., 1], second_weight[:, None, :], jnp.float32(0.0)
    )

    def per_slot(values):
        out = jnp.sum(jnp.where(match, values[:, :, None, :], jnp.float32(0.0)), axis=3)
        return jnp.swapaxes(out, 0, 1).reshape(local_experts, attn * cap, 1)

    slot_weight = per_slot(row_weight)
    slot_scale = per_slot(jnp.broadcast_to(scale[:, None, :], row_weight.shape))

    slab_rows = pick_rows(selector, gathered, width_local, local_experts)
    gate_part = jnp.einsum("end,edf->enf", slab_rows, w_gate, preferred_element_type=jnp.float32) * slot_scale
    up_part = jnp.einsum("end,edf->enf", slab_rows, w_up, preferred_element_type=jnp.float32) * slot_scale
    activation = (jax.nn.silu(gate_part) * up_part * slot_weight).astype(jnp.bfloat16)
    total = reduce_all(activation, selector, w_down, sizes)
    return (hidden_state + total).astype(jnp.bfloat16)


def solution(mesh):
    sizes = grid_of(mesh.shape["attn"], mesh.shape["expert"])
    return jax.shard_map(
        functools.partial(on_device, sizes),
        mesh=mesh,
        in_specs=(
            P("attn", "expert"),
            P("attn", "expert"),
            P("attn", "expert", None, None),
            P("attn", "expert", None, None),
            P("attn", "expert"),
            P("attn", "expert"),
            P("attn"),
            P("expert"),
            P("expert", None),
            P("attn", None),
            P("expert", None, "attn"),
            P("expert", None, "attn"),
            P("expert", "attn", None),
        ),
        out_specs=P("attn", "expert"),
        check_vma=False,
    )
```
